32 devices in a mesh: event: 8 (over z, core), mesh: 4 (over y, x).
Axes of the slice: x: 2, y: 2, z: 4, core: 2. Of those that a mesh axis runs over, the one named last changes fastest.
Arguments:
- forward_start: float32 [8, 3, 125, 512], P('event', None, None, 'mesh'), may hold values from -6 to 6
- adjoint_start: float32 [8, 3, 125, 512], P('event', None, None, 'mesh'), may hold values from -6 to 6
- stiffness: float32 [125, 125], replicated
- projection: float32 [125, 64], replicated, may hold values from -0.5 to 0.5
- material: float32 [8, 512], P('event', 'mesh'), may hold values from 0.5 to 2
- neighbours: int32 [8, 6, 512], P('event', None, 'mesh'), may hold values from 0 to 511, as said below
- destinations: int32 [8, 512], P('event', 'mesh'), may hold values from 0 to 127
- counts: int32 [8, 4], P('event', 'mesh'), may hold values from 32 to 128, as said below
- smoothing: float32 [4, 128], P(None, ('event', 'mesh')), may hold values from 0.02 to 0.12
Outputs:
- forward_final: float32 [8, 3, 125, 512], P('event', None, None, 'mesh')
- tiles: float32 [64, 128], P(None, ('event', 'mesh'))
The draws below stay inside these ranges and needn't reach their ends.
Inputs may be any that keep to these rules, and one draw needn't show every extreme that they name: `counts`: in every event one partition holds exactly 128 live elements and another exactly 32; live elements fill a partition's first slots. `neighbours`: A neighbour slot lies in the element's own partition, or in the previous or next partition of the same event (wrapping around), and then among that partition's first 32 slots.
All inputs are finite; a program needn't handle non-finite values.
Results may differ from the reference program's by a relative error of at most 0.0003.
Values sent between devices are 32-bit elements; how exact they have to be, the bound alone decides.
A program may use at most 64 MiB of HBM per device.

```python
import math
import jax
import jax.numpy as jnp
from jax import lax

NODES = 125
KNODES = 64
COMP = 3
ECAP = 128
TILE_DEV = 4
STEPS = 2
BND = 32
EVENTS = 8
PARTITIONS = 4
ELEM = 512
NTILE = 128


def draw_stiffness(key, part):
    sample_key = jax.random.fold_in(key, 37)
    factor = jax.random.normal(sample_key, (NODES, NODES), jnp.float32)
    gram_matrix = jnp.dot(factor, factor.T, precision=lax.Precision.HIGHEST) / NODES
    return 0.25 * gram_matrix + 0.1 * jnp.eye(NODES, dtype=jnp.float32)


def draw_counts(key, part):
    first_key, second_key = jax.random.split(jax.random.fold_in(key, 11))
    drawn = jax.random.randint(first_key, (EVENTS, PARTITIONS), ECAP // 4, ECAP + 1)
    fullest = jax.random.randint(second_key, (EVENTS, 1), 0, PARTITIONS)
    columns = jnp.arange(PARTITIONS)[None, :]
    drawn = jnp.where(columns == fullest, ECAP, drawn)
    drawn = jnp.where(columns == (fullest + 1) % PARTITIONS, ECAP // 4, drawn)
    return drawn.astype(jnp.int32)


def draw_neighbours(key, part):
    side_key, near_key, far_key = jax.random.split(jax.random.fold_in(key, 23), 3)
    grid_shape = (EVENTS, 6, ELEM)
    which_side = jax.random.randint(side_key, grid_shape, 0, 4)
    near_slot = jax.random.randint(near_key, grid_shape, 0, ECAP)
    far_slot = jax.random.randint(far_key, grid_shape, 0, BND)
    partition = jnp.arange(ELEM)[None, None, :] // ECAP
    offset = jnp.where(which_side == 2, -1, jnp.where(which_side == 3, 1, 0))
    target = (partition + offset + PARTITIONS) % PARTITIONS
    local_slot = jnp.where(which_side >= 2, far_slot, near_slot)
    result = target * ECAP + local_slot
    result = result.at[:, 0, ELEM - 1].set(ELEM - 1)
    result = result.at[:, 1, 1].set(0)
    return result.astype(jnp.int32)


def with_ends(values, key, least, high):
    shape = values.shape
    place = [jax.random.randint(jax.random.fold_in(key, axis), (), 0, shape[axis]) for axis in range(len(shape))]
    values = values.at[tuple(place)].set(least)
    longest = shape.index(max(shape))
    place[longest] = (place[longest] + 1) % shape[longest]
    return values.at[tuple(place)].set(high)


def block_levels(own_key, dims, pieces, least, high):
    level, own = 1.0, jax.random.fold_in(own_key, 6)
    for axis_at, shards_of in pieces:
        steps = jnp.exp(jax.random.uniform(jax.random.fold_in(own, axis_at), (shards_of,), jnp.float32, least / len(pieces), high / len(pieces)))
        level = level * jnp.repeat(steps, dims[axis_at] // shards_of).reshape([-1 if axis == axis_at else 1 for axis in range(len(dims))])
    return level


def normal_values(stream_key, dims, spread, reach, pieces=(), held_as=jnp.bfloat16):
    level = block_levels(stream_key, dims, pieces, -0.22, 0.18) if pieces else 1.0
    values = jax.random.normal(stream_key, dims, jnp.float32) * spread * level
    return jnp.minimum(jnp.maximum(values, -reach), reach).astype(held_as)


def setup_inputs(seed: int = 0) -> dict:
    key_of = jax.random.split(jax.random.key(seed), 10)
    return {
        "forward_start": normal_values(key_of[0], (EVENTS, COMP, NODES, ELEM), 1.0, 6.0, ((0, 8), (3, 4)), jnp.float32),
        "adjoint_start": normal_values(key_of[1], (EVENTS, COMP, NODES, ELEM), 1.0, 6.0, ((0, 8), (3, 4)), jnp.float32),
        "stiffness": draw_stiffness(jax.random.fold_in(key_of[9], 71), 0),
        "projection": normal_values(key_of[3], (NODES, KNODES), NODES ** -0.5, 0.5, (), jnp.float32),
        "material": jnp.clip(jnp.exp(math.log(2.0) - 1.3862944 * jax.random.uniform(key_of[4], (EVENTS, ELEM), jnp.float32) ** block_levels(key_of[4], (EVENTS, ELEM), ((0, 8), (1, 4)), -0.2, 0.2)), 0.5, 2.0),
        "neighbours": draw_neighbours(jax.random.fold_in(key_of[9], 71), 0),
        "destinations": with_ends(jax.random.randint(key_of[6], (EVENTS, ELEM), 0, NTILE), jax.random.fold_in(key_of[6], 1), 0, NTILE - 1).astype(jnp.int32),
        "counts": draw_counts(jax.random.fold_in(key_of[9], 71), 0),
        "smoothing": jnp.clip(jnp.exp(math.log(0.12) - 1.7917595 * jax.random.uniform(key_of[8], (4, NTILE), jnp.float32) ** block_levels(key_of[8], (4, NTILE), ((1, 32),), -0.2, 0.2)), 0.02, 0.12),
    }


time_square = 0.4
penalty = 0.5
partner_face = (1, 0, 3, 2, 5, 4)

def element_faces(field):
    elements = field.shape[-1]
    cube = field.reshape(3, 5, 5, 5, elements)
    sheets = [cube[:, 0], cube[:, 4], cube[:, :, 0], cube[:, :, 4], cube[:, :, :, 0], cube[:, :, :, 4]]
    return jnp.stack(sheets).reshape(6, 3, 25, elements)

def lift_faces(jumps):
    elements = jumps.shape[-1]
    sheets = jumps.reshape(6, 3, 5, 5, elements)
    keep = (0, 0)
    lifted = jnp.pad(sheets[0][:, None], (keep, (0, 4), keep, keep, keep))
    lifted = lifted + jnp.pad(sheets[1][:, None], (keep, (4, 0), keep, keep, keep))
    lifted = lifted + jnp.pad(sheets[2][:, :, None], (keep, keep, (0, 4), keep, keep))
    lifted = lifted + jnp.pad(sheets[3][:, :, None], (keep, keep, (4, 0), keep, keep))
    lifted = lifted + jnp.pad(sheets[4][:, :, :, None], (keep, keep, keep, (0, 4), keep))
    lifted = lifted + jnp.pad(sheets[5][:, :, :, None], (keep, keep, keep, (4, 0), keep))
    return lifted.reshape(3, 125, elements)

def apply_stiffness(stiffness, field):
    return jnp.einsum('nm,cme->cne', stiffness, field, precision=lax.Precision.HIGHEST)

def pick_faces(faces, neighbour_rows):
    return jnp.stack([jnp.take(faces[partner_face[face]], neighbour_rows[face], axis=2) for face in range(6)])

def advance(field, previous, strain, across, own_faces, material_row, live):
    force = -material_row[None, None, :] * strain + penalty * lift_faces(across - own_faces)
    return live[None, None, :] * (2.0 * field - previous + time_square * force)

def node_laplace(values, coefs):
    width = values.shape[-1]
    cube = values.reshape(4, 4, 4, width)
    padded = jnp.pad(cube, ((1, 1), (1, 1), (1, 1), (0, 0)))
    first_dir = padded[2:, 1:-1, 1:-1] + padded[:-2, 1:-1, 1:-1] - 2.0 * cube
    second_dir = padded[1:-1, 2:, 1:-1] + padded[1:-1, :-2, 1:-1] - 2.0 * cube
    third_dir = padded[1:-1, 1:-1, 2:] + padded[1:-1, 1:-1, :-2] - 2.0 * cube
    summed = coefs[0] * first_dir + coefs[1] * second_dir + coefs[2] * third_dir
    return summed.reshape(64, width)

def smooth_columns(values, coefs):
    middle = values[:, 1:-1]
    chain = values[:, :-2] + values[:, 2:] - 2.0 * middle
    return middle + coefs[0] * chain + node_laplace(middle, coefs[1:])

def reference(forward_start, adjoint_start, stiffness, projection, material, neighbours, destinations, counts, smoothing):
    scale = math.sqrt(TILE_DEV / ECAP) / STEPS

    def one_event(summed, inputs):
        forward_row, adjoint_row, material_row, neighbour_rows, destination_row, count_row = inputs
        slots = jnp.arange(ECAP, dtype=jnp.int32)
        live = (slots[None, :] < count_row[:, None]).reshape(ELEM).astype(jnp.float32)
        forward = forward_row * live[None, None, :]
        adjoint = adjoint_row * live[None, None, :]
        forward_prev, adjoint_prev = (forward, adjoint)
        kernel = jnp.zeros((NODES, ELEM), jnp.float32)
        for step_index in range(STEPS):
            strain_forward = apply_stiffness(stiffness, forward)
            strain_adjoint = apply_stiffness(stiffness, adjoint)
            kernel = kernel + lax.optimization_barrier(jnp.sum(forward * strain_adjoint, axis=0))
            faces_forward = element_faces(forward)
            faces_adjoint = element_faces(adjoint)
            across_forward = pick_faces(faces_forward, neighbour_rows)
            across_adjoint = pick_faces(faces_adjoint, neighbour_rows)
            next_forward = advance(forward, forward_prev, strain_forward, across_forward, faces_forward, material_row, live)
            next_adjoint = advance(adjoint, adjoint_prev, strain_adjoint, across_adjoint, faces_adjoint, material_row, live)
            forward_prev, forward = (forward, next_forward)
            adjoint_prev, adjoint = (adjoint, next_adjoint)
        blocks = jnp.dot(projection.T, kernel, precision=lax.Precision.HIGHEST) * scale
        summed = summed.at[:, destination_row].add(blocks)
        return (summed, forward)
    summed, finals = lax.scan(one_event, jnp.zeros((KNODES, NTILE), jnp.float32), (forward_start, adjoint_start, material, neighbours, destinations, counts))
    tiles = summed
    for pass_index in range(2):
        padded = jnp.pad(tiles, ((0, 0), (1, 1)))
        tiles = smooth_columns(padded, smoothing)
    return (finals, tiles)
```

```python
import functools
import math

import jax
import jax.numpy as jnp
from jax import lax
from jax.experimental import pallas as pl
from jax.experimental.pallas import tpu as pltpu
from jax.sharding import PartitionSpec as P

STEPS = 2
time_square = 0.4
penalty = 0.5

PAD = 8
ROWS = 128
NODES = 125
SHIFT = (100, -100, 20, -20, 4, -4)
MESH = pl.DeviceIdType.MESH
f32 = jnp.float32
bf16 = jnp.bfloat16


def on_face(face, node):
    i, j, k = node // 25, (node // 5) % 5, node % 5
    return (i == 0, i == 4, j == 0, j == 4, k == 0, k == 4)[face]


TILE_FACES = [
    [f for f in range(6) if any(on_face(f, n) for n in range(8 * t, min(8 * t + 8, NODES)))]
    for t in range(ROWS // 8)
]


def split(x):
    high = x.astype(bf16)
    return high, (x - high.astype(f32)).astype(bf16)


def mm(a, b, dims=((1,), (0,))):
    return lax.dot_general(a, b, (dims, ((), ())), preferred_element_type=f32)


def pick(x, index):
    return jnp.take_along_axis(x, index, axis=1, mode="promise_in_bounds")


def kernel(
    m_size, e_size,
    fwd_in, adj_in, stiff_in, proj_in, mat_in, nb_in, dest_in, count_in, smooth_in,
    fwd_out, tiles_out,
    F, N, K, S, W, IDX, LIVE, send, rim, rim2, coef, coef_in, msg, part, got, mine, got2,
    rim_s, rim_r, rim2_s, rim2_r, coef_s, coef_r, a_s, a_r, b_s, b_r,
):
    me = lax.axis_index("mesh")
    ev = lax.axis_index("event")
    total = m_size * e_size
    lin = ev * m_size + me
    after = lax.rem(me + 1, m_size)
    before = lax.rem(me + m_size - 1, m_size)
    nxt = lax.rem(lin + 1, total)
    prv = lax.rem(lin + total - 1, total)
    lin_id = lambda d: (lax.div(d, m_size), lax.rem(d, m_size))

    barrier = pltpu.get_barrier_semaphore()
    partners = [(ev, lax.rem(me + j, m_size)) for j in range(1, m_size)]
    partners += [(lax.rem(ev + j, e_size), me) for j in range(1, e_size)]
    partners += [lin_id(nxt), lin_id(prv)]
    for device in partners:
        pl.semaphore_signal(barrier, inc=1, device_id=device, device_id_type=MESH)

    lane = lax.broadcasted_iota(jnp.int32, (1, 128), 1)
    live = jnp.where(lane < count_in[0:1, 0:1], 1.0, 0.0).astype(f32)
    LIVE[...] = jnp.broadcast_to(live, (8, 128))
    zero8 = jnp.zeros((PAD, 128), f32)
    for fc in range(6):
        source = fwd_in if fc < 3 else adj_in
        F[fc, 0:PAD, :] = zero8
        F[fc, 128:136, :] = zero8
        F[fc, 136:144, :] = zero8
        F[fc, PAD : PAD + NODES, :] = source[0, fc % 3] * live

    def pack(base):
        wide = [F[base + c, PAD : PAD + ROWS, :] for c in range(3)]
        head = jnp.where(
            lane < 32,
            wide[0][:96],
            jnp.where(lane < 64, pltpu.roll(wide[1][:96], 32, 1), pltpu.roll(wide[2][:96], 64, 1)),
        )
        tail = pltpu.roll(jnp.concatenate([w[96:] for w in wide], axis=0), 96, 1)
        return jnp.where(lane < 96, head, tail)

    send[0] = pack(0)
    send[1] = pack(3)
    coef[...] = jnp.zeros((8, 128), f32)
    coef[0:4, 0:4] = smooth_in[...]

    pl.semaphore_wait(barrier, len(partners))

    def remote(src, dst, s, r, device):
        copy = pltpu.make_async_remote_copy(
            src_ref=src, dst_ref=dst, send_sem=s, recv_sem=r, device_id=device, device_id_type=MESH
        )
        copy.start()
        return copy

    rim_copies = [
        [
            remote(send.at[f], rim.at[f, 0, pl.ds(PAD, 96)], rim_s.at[f, 0], rim_r.at[f, 0], (ev, after)),
            remote(send.at[f], rim.at[f, 1, pl.ds(PAD, 96)], rim_s.at[f, 1], rim_r.at[f, 1], (ev, before)),
        ]
        for f in range(2)
    ]
    coef_copies = [
        remote(coef, coef_in.at[0], coef_s.at[0], coef_r.at[0], lin_id(nxt)),
        remote(coef, coef_in.at[1], coef_s.at[1], coef_r.at[1], lin_id(prv)),
    ]

    node = lax.broadcasted_iota(jnp.int32, (ROWS, 128), 0).astype(f32)
    i = jnp.floor((node + 0.5) / 25.0)
    rest = node - 25.0 * i
    j = jnp.floor((rest + 0.5) / 5.0)
    k = rest - 5.0 * j
    count = jnp.zeros((ROWS, 128), f32)
    for f, test in enumerate((i == 0.0, i == 4.0, j == 0.0, j == 4.0, k == 0.0, k == 4.0)):
        mask = jnp.where(test & (node < NODES - 0.5), 1.0, 0.0).astype(f32)
        W[f] = mask
        count = count + mask
    W[6] = count
    nb = nb_in[0]
    target = lax.shift_right_logical(nb, 7)
    slot = nb & 127
    relative = lax.rem(target - me + m_size, m_size)
    for f in range(6):
        IDX[f] = jnp.broadcast_to(slot[f : f + 1], (8, 128))
        IDX[6 + f] = jnp.broadcast_to(relative[f : f + 1], (8, 128))
    S[...] = jnp.zeros((ROWS, ROWS), f32)
    S[0:NODES, 0:NODES] = stiff_in[...]
    s_hi, s_lo = split(S[...])
    material = mat_in[...]

    def strain(base):
        wide = jnp.concatenate([F[base + c, PAD : PAD + ROWS, :] for c in range(3)], axis=1)
        hi, lo = split(wide)
        both = mm(s_hi, hi) + (mm(s_hi, lo) + mm(s_lo, hi))
        return [both[:, 128 * c : 128 * (c + 1)] for c in range(3)]

    def own_pass(base):
        def body(c, carry):
            for t in range(ROWS // 8):
                acc = jnp.zeros((8, 128), f32)
                for f in TILE_FACES[t]:
                    x = F[base + c, 8 * t + PAD + SHIFT[f] : 8 * t + 2 * PAD + SHIFT[f], :]
                    g = pick(x, IDX[f])
                    acc = acc + jnp.where(IDX[6 + f] == 0, g, 0.0) * W[f, 8 * t : 8 * t + 8, :]
                v = F[base + c, 8 * t + PAD : 8 * t + 2 * PAD, :]
                acc = acc - W[6, 8 * t : 8 * t + 8, :] * v
                N[base + c, 8 * t : 8 * t + 8, :] = (
                    N[base + c, 8 * t : 8 * t + 8, :] + (time_square * penalty) * acc
                )
            return carry

        lax.fori_loop(0, 3, body, 0)

    def unpack(ref):
        pieces = [
            pltpu.roll(ref[PAD + 32 * c : PAD + 32 * c + 32, :], 32 * (c + 1), 1) for c in range(3)
        ]
        ref[PAD + 96 : PAD + 128, :] = jnp.where(
            lane < 32, pieces[0], jnp.where(lane < 64, pieces[1], pieces[2])
        )
        ref[0:PAD, :] = zero8
        ref[PAD + 128 : PAD + 136, :] = zero8

    def rim_pass(base, ref, store):
        def body(c, carry):
            live8 = LIVE[...]
            for t in range(ROWS // 8):
                acc = jnp.zeros((8, 128), f32)
                for f in TILE_FACES[t]:
                    low = 8 * t + PAD + SHIFT[f]
                    at = (IDX[f] & 31) + 32 * c
                    r = IDX[6 + f]
                    g = jnp.where(
                        r == 1, pick(ref[1, low : low + 8, :], at), pick(ref[0, low : low + 8, :], at)
                    )
                    acc = acc + jnp.where(r == 0, 0.0, g) * W[f, 8 * t : 8 * t + 8, :]
                old = N[base + c, 8 * t : 8 * t + 8, :]
                store(c, t, live8 * (old + (time_square * penalty) * acc))
            return carry

        lax.fori_loop(0, 3, body, 0)

    st_f = strain(0)
    st_a = strain(3)
    energy = jnp.zeros((ROWS, 128), f32)
    for c in range(3):
        vf = F[c, PAD : PAD + ROWS, :]
        energy = energy + vf * st_a[c]
        N[c] = vf - time_square * material * st_f[c]
        N[3 + c] = F[3 + c, PAD : PAD + ROWS, :] - time_square * material * st_a[c]
    K[...] = energy
    own_pass(0)
    own_pass(3)

    def keep(base):
        def store(c, t, value):
            at = pl.ds(8 * t + PAD, 8)
            if base == 0:
                N[c, 8 * t : 8 * t + 8, :] = 2.0 * value - F[c, at, :]
            F[base + c, at, :] = value

        return store

    for f in range(2):
        for side in range(2):
            rim_copies[f][side].wait_recv()
            unpack(rim.at[f, side])
        rim_pass(3 * f, rim.at[f], keep(3 * f))
        if f == 0:
            send[2] = pack(0)
            rim2_copies = [
                remote(send.at[2], rim2.at[0, pl.ds(PAD, 96)], rim2_s.at[0], rim2_r.at[0], (ev, after)),
                remote(send.at[2], rim2.at[1, pl.ds(PAD, 96)], rim2_s.at[1], rim2_r.at[1], (ev, before)),
            ]

    st_a = strain(3)
    energy = K[...]
    for c in range(3):
        energy = energy + F[c, PAD : PAD + ROWS, :] * st_a[c]
    elements = fwd_in.shape[-1]
    width = smooth_in.shape[1]
    scale = math.sqrt(width / elements) / STEPS
    twin = jnp.concatenate([proj_in[...], proj_in[...]], axis=1)
    K[...] = energy
    blocks = lax.dot_general(
        twin, K[0:NODES, :], (((0,), (0,)), ((), ())),
        preferred_element_type=f32, precision=lax.Precision.HIGHEST,
    ) * scale
    b_hi, b_lo = split(blocks)
    rows = total * width
    row = lax.broadcasted_iota(jnp.int32, (rows, 128), 0)
    owner = lax.div(row, width)
    tile = width * (lax.rem(owner, e_size) * m_size + lax.div(owner, e_size)) + lax.rem(row, width)
    dest = dest_in[...]
    nt = ((1,), (1,))

    def spread(offset):
        hot = jnp.where(tile + offset == dest, 1.0, 0.0).astype(f32).astype(bf16)
        return mm(hot, b_hi, nt) + mm(hot, b_lo, nt)

    packed = jnp.where(lane < 64, spread(-2), spread(2))
    msg[...] = packed.reshape(m_size, e_size, width, 128)
    a_copies = [
        remote(msg.at[lax.rem(me + o, m_size)], got.at[o - 1], a_s.at[o - 1], a_r.at[o - 1],
               (ev, lax.rem(me + o, m_size)))
        for o in range(1, m_size)
    ]

    st_f = strain(0)
    for c in range(3):
        N[c] = N[c] - time_square * material * st_f[c]
    own_pass(0)

    for copy in a_copies:
        copy.wait_recv()
    mine_sum = msg[me]
    for o in range(m_size - 1):
        mine_sum = mine_sum + got[o]
    part[...] = mine_sum
    b_copies = [
        remote(part.at[lax.rem(ev + o, e_size)], got2.at[o - 1], b_s.at[o - 1], b_r.at[o - 1],
               (lax.rem(ev + o, e_size), me))
        for o in range(1, e_size)
    ]

    for side in range(2):
        rim2_copies[side].wait_recv()
        unpack(rim2.at[side])

    def final(c, t, value):
        size = min(8, NODES - 8 * t)
        fwd_out[0, c, 8 * t : 8 * t + size, :] = value[:size]

    rim_pass(0, rim2, final)

    for copy in coef_copies:
        copy.wait_recv()
    own_coef = pltpu.roll(coef[...], 2, 1)
    left = jnp.where(lin > 0, coef_in[0], 0.0)
    right = jnp.where(lin < total - 1, coef_in[1], 0.0)
    left = jnp.where(lane < 2, pltpu.roll(left, 126, 1), 0.0)
    right = pltpu.roll(right, 6, 1)
    coefs = own_coef + left + right

    for copy in b_copies:
        copy.wait_recv()
    summed = part[ev]
    for o in range(e_size - 1):
        summed = summed + got2[o]
    mine[...] = jnp.zeros((128, 128), f32)
    mine[0:width, :] = summed
    turned = mine[...].T
    x = jnp.where(lane < 4, turned[0:64], pltpu.roll(turned[64:128], 4, 1))
    x = jnp.where(lane < 8, x, 0.0)
    r64 = lax.broadcasted_iota(jnp.int32, (64, 128), 0)
    for _ in range(2):
        chain = pltpu.roll(x, 1, 1) + pltpu.roll(x, 127, 1) - 2.0 * x
        new = x + coefs[0:1] * chain
        for d, stride in ((1, 16), (2, 4), (3, 1)):
            digit = lax.shift_right_logical(r64, {16: 4, 4: 2, 1: 0}[stride]) & 3
            up = jnp.where(digit == 0, 0.0, pltpu.roll(x, stride, 0))
            down = jnp.where(digit == 3, 0.0, pltpu.roll(x, 64 - stride, 0))
            new = new + coefs[d : d + 1] * (up + down - 2.0 * x)
        x = jnp.where(lane < 8, new, 0.0)
    tiles_out[...] = pltpu.roll(x, 126, 1)[:, 0:width]

    for copy in rim_copies[0] + rim_copies[1] + rim2_copies + coef_copies + a_copies + b_copies:
        copy.wait_send()


def solution(mesh):
    m_size, e_size = mesh.shape["mesh"], mesh.shape["event"]
    in_specs = (
        P("event", None, None, "mesh"),
        P("event", None, None, "mesh"),
        P(),
        P(),
        P("event", "mesh"),
        P("event", None, "mesh"),
        P("event", "mesh"),
        P("event", "mesh"),
        P(None, ("event", "mesh")),
    )
    out_specs = (P("event", None, None, "mesh"), P(None, ("event", "mesh")))

    def per_device(*args):
        fwd, smoothing = args[0], args[-1]
        width = smoothing.shape[1]
        dma = pltpu.SemaphoreType.DMA
        vmem = pl.BlockSpec(memory_space=pltpu.VMEM)
        return pl.pallas_call(
            functools.partial(kernel, m_size, e_size),
            out_shape=(
                jax.ShapeDtypeStruct(fwd.shape, f32),
                jax.ShapeDtypeStruct((64, width), f32),
            ),
            in_specs=[vmem] * len(args),
            out_specs=(vmem, vmem),
            scratch_shapes=[
                pltpu.VMEM((6, 144, 128), f32),
                pltpu.VMEM((6, ROWS, 128), f32),
                pltpu.VMEM((ROWS, 128), f32),
                pltpu.VMEM((ROWS, ROWS), f32),
                pltpu.VMEM((7, ROWS, 128), f32),
                pltpu.VMEM((12, 8, 128), jnp.int32),
                pltpu.VMEM((8, 128), f32),
                pltpu.VMEM((3, 96, 128), f32),
                pltpu.VMEM((2, 2, 144, 128), f32),
                pltpu.VMEM((2, 144, 128), f32),
                pltpu.VMEM((8, 128), f32),
                pltpu.VMEM((2, 8, 128), f32),
                pltpu.VMEM((m_size, e_size, width, 128), f32),
                pltpu.VMEM((e_size, width, 128), f32),
                pltpu.VMEM((m_size - 1, e_size, width, 128), f32),
                pltpu.VMEM((128, 128), f32),
                pltpu.VMEM((e_size - 1, width, 128), f32),
                dma((2, 2)), dma((2, 2)), dma((2,)), dma((2,)), dma((2,)), dma((2,)),
                dma((m_size - 1,)), dma((m_size - 1,)), dma((e_size - 1,)), dma((e_size - 1,)),
            ],
            compiler_params=pltpu.CompilerParams(collective_id=0, has_side_effects=True),
        )(*args)

    return jax.shard_map(
        per_device, mesh=mesh, in_specs=in_specs, out_specs=out_specs, check_vma=False
    )
```

```python
import functools
import math

import jax
import jax.numpy as jnp
from jax import lax
from jax.experimental import pallas as pl
from jax.experimental.pallas import tpu as pltpu
from jax.sharding import PartitionSpec as P

STEPS = 2
time_square = 0.4
penalty = 0.5

PAD = 8
ROWS = 128
NODES = 125
SHIFT = (100, -100, 20, -20, 4, -4)
MESH = pl.DeviceIdType.MESH
f32 = jnp.float32
bf16 = jnp.bfloat16


def on_face(face, node):
    i, j, k = node // 25, (node // 5) % 5, node % 5
    return (i == 0, i == 4, j == 0, j == 4, k == 0, k == 4)[face]


TILE_FACES = [
    [f for f in range(6) if any(on_face(f, n) for n in range(8 * t, min(8 * t + 8, NODES)))]
    for t in range(ROWS // 8)
]


def split(x):
    high = x.astype(bf16)
    return high, (x - high.astype(f32)).astype(bf16)


def mm(a, b, dims=((1,), (0,))):
    return lax.dot_general(a, b, (dims, ((), ())), preferred_element_type=f32)


def pick(x, index):
    return jnp.take_along_axis(x, index, axis=1, mode="promise_in_bounds")


def kernel(
    m_size, e_size,
    fwd_in, adj_in, stiff_in, proj_in, mat_in, nb_in, dest_in, count_in, smooth_in,
    fwd_out, tiles_out,
    F, N, K, S, W, IDX, LIVE, send, rim, rim2, coef, coef_in, msg, part, got, mine, got2,
    in_s, out_s, rim_s, rim_r, rim2_s, rim2_r, coef_s, coef_r, a_s, a_r, b_s, b_r,
):
    me = lax.axis_index("mesh")
    ev = lax.axis_index("event")
    total = m_size * e_size
    lin = ev * m_size + me
    after = lax.rem(me + 1, m_size)
    before = lax.rem(me + m_size - 1, m_size)
    nxt = lax.rem(lin + 1, total)
    prv = lax.rem(lin + total - 1, total)
    lin_id = lambda d: (lax.div(d, m_size), lax.rem(d, m_size))

    loads = []
    for fc in range(6):
        source = fwd_in if fc < 3 else adj_in
        load = pltpu.make_async_copy(
            source.at[pl.ds(NODES * (fc % 3), NODES), 0], F.at[fc, pl.ds(PAD, NODES)], in_s.at[fc]
        )
        load.start()
        loads.append(load)

    barrier = pltpu.get_barrier_semaphore()
    partners = [(ev, lax.rem(me + j, m_size)) for j in range(1, m_size)]
    partners += [(lax.rem(ev + j, e_size), me) for j in range(1, e_size)]
    partners += [lin_id(nxt), lin_id(prv)]
    for device in partners:
        pl.semaphore_signal(barrier, inc=1, device_id=device, device_id_type=MESH)

    lane = lax.broadcasted_iota(jnp.int32, (1, 128), 1)
    live = jnp.where(lane < count_in[0:1, 0:1], 1.0, 0.0).astype(f32)
    LIVE[...] = jnp.broadcast_to(live, (8, 128))
    zero8 = jnp.zeros((PAD, 128), f32)
    for fc in range(6):
        F[fc, 0:PAD, :] = zero8
        F[fc, PAD + NODES : 144, :] = jnp.zeros((144 - PAD - NODES, 128), f32)

    def pack(base):
        wide = [F[base + c, PAD : PAD + ROWS, :] for c in range(3)]
        head = jnp.where(
            lane < 32,
            wide[0][:96],
            jnp.where(lane < 64, pltpu.roll(wide[1][:96], 32, 1), pltpu.roll(wide[2][:96], 64, 1)),
        )
        tail = pltpu.roll(jnp.concatenate([w[96:] for w in wide], axis=0), 96, 1)
        return jnp.where(lane < 96, head, tail)

    for f in range(2):
        for load in loads[3 * f : 3 * f + 3]:
            load.wait()
        send[f] = pack(3 * f)
    coef[...] = jnp.zeros((8, 128), f32)
    coef[0:4, 0:4] = smooth_in[...]

    pl.semaphore_wait(barrier, len(partners))

    def remote(src, dst, s, r, device):
        copy = pltpu.make_async_remote_copy(
            src_ref=src, dst_ref=dst, send_sem=s, recv_sem=r, device_id=device, device_id_type=MESH
        )
        copy.start()
        return copy

    rim_copies = [
        [
            remote(send.at[f], rim.at[f, 0, pl.ds(PAD, 96)], rim_s.at[f, 0], rim_r.at[f, 0], (ev, after)),
            remote(send.at[f], rim.at[f, 1, pl.ds(PAD, 96)], rim_s.at[f, 1], rim_r.at[f, 1], (ev, before)),
        ]
        for f in range(2)
    ]
    coef_copies = [
        remote(coef, coef_in.at[0], coef_s.at[0], coef_r.at[0], lin_id(nxt)),
        remote(coef, coef_in.at[1], coef_s.at[1], coef_r.at[1], lin_id(prv)),
    ]

    for fc in range(6):
        F[fc, PAD : PAD + NODES, :] = F[fc, PAD : PAD + NODES, :] * live

    node = lax.broadcasted_iota(jnp.int32, (ROWS, 128), 0).astype(f32)
    i = jnp.floor((node + 0.5) / 25.0)
    rest = node - 25.0 * i
    j = jnp.floor((rest + 0.5) / 5.0)
    k = rest - 5.0 * j
    count = jnp.zeros((ROWS, 128), f32)
    for f, test in enumerate((i == 0.0, i == 4.0, j == 0.0, j == 4.0, k == 0.0, k == 4.0)):
        mask = jnp.where(test & (node < NODES - 0.5), 1.0, 0.0).astype(f32)
        W[f] = mask
        count = count + mask
    W[6] = count
    nb = nb_in[:, 0, :]
    target = lax.shift_right_logical(nb, 7)
    slot = nb & 127
    relative = lax.rem(target - me + m_size, m_size)
    for f in range(6):
        IDX[f] = jnp.broadcast_to(slot[f : f + 1], (8, 128))
        IDX[6 + f] = jnp.broadcast_to(relative[f : f + 1], (8, 128))
    S[...] = jnp.zeros((ROWS, ROWS), f32)
    S[0:NODES, 0:NODES] = stiff_in[...]
    s_hi, s_lo = split(S[...])
    material = mat_in[...]

    def strain(base):
        wide = jnp.concatenate([F[base + c, PAD : PAD + ROWS, :] for c in range(3)], axis=1)
        hi, lo = split(wide)
        both = mm(s_hi, hi) + (mm(s_hi, lo) + mm(s_lo, hi))
        return [both[:, 128 * c : 128 * (c + 1)] for c in range(3)]

    def own_pass(base):
        def body(c, carry):
            for t in range(ROWS // 8):
                acc = jnp.zeros((8, 128), f32)
                for f in TILE_FACES[t]:
                    x = F[base + c, 8 * t + PAD + SHIFT[f] : 8 * t + 2 * PAD + SHIFT[f], :]
                    g = pick(x, IDX[f])
                    acc = acc + jnp.where(IDX[6 + f] == 0, g, 0.0) * W[f, 8 * t : 8 * t + 8, :]
                v = F[base + c, 8 * t + PAD : 8 * t + 2 * PAD, :]
                acc = acc - W[6, 8 * t : 8 * t + 8, :] * v
                N[base + c, 8 * t : 8 * t + 8, :] = (
                    N[base + c, 8 * t : 8 * t + 8, :] + (time_square * penalty) * acc
                )
            return carry

        lax.fori_loop(0, 3, body, 0)

    def unpack(ref):
        pieces = [
            pltpu.roll(ref[PAD + 32 * c : PAD + 32 * c + 32, :], 32 * (c + 1), 1) for c in range(3)
        ]
        ref[PAD + 96 : PAD + 128, :] = jnp.where(
            lane < 32, pieces[0], jnp.where(lane < 64, pieces[1], pieces[2])
        )
        ref[0:PAD, :] = zero8
        ref[PAD + 128 : PAD + 136, :] = zero8

    def rim_pass(base, ref, store):
        def body(c, carry):
            live8 = LIVE[...]
            for t in range(ROWS // 8):
                acc = jnp.zeros((8, 128), f32)
                for f in TILE_FACES[t]:
                    low = 8 * t + PAD + SHIFT[f]
                    at = (IDX[f] & 31) + 32 * c
                    r = IDX[6 + f]
                    g = jnp.where(
                        r == 1, pick(ref[1, low : low + 8, :], at), pick(ref[0, low : low + 8, :], at)
                    )
                    acc = acc + jnp.where(r == 0, 0.0, g) * W[f, 8 * t : 8 * t + 8, :]
                old = N[base + c, 8 * t : 8 * t + 8, :]
                store(c, t, live8 * (old + (time_square * penalty) * acc))
            return carry

        lax.fori_loop(0, 3, body, 0)

    st_f = strain(0)
    st_a = strain(3)
    energy = jnp.zeros((ROWS, 128), f32)
    for c in range(3):
        vf = F[c, PAD : PAD + ROWS, :]
        energy = energy + vf * st_a[c]
        N[c] = vf - time_square * material * st_f[c]
        N[3 + c] = F[3 + c, PAD : PAD + ROWS, :] - time_square * material * st_a[c]
    K[...] = energy
    own_pass(0)
    own_pass(3)

    def keep(base):
        def store(c, t, value):
            at = pl.ds(8 * t + PAD, 8)
            if base == 0:
                N[c, 8 * t : 8 * t + 8, :] = 2.0 * value - F[c, at, :]
            F[base + c, at, :] = value

        return store

    for f in range(2):
        for side in range(2):
            rim_copies[f][side].wait_recv()
            unpack(rim.at[f, side])
        rim_pass(3 * f, rim.at[f], keep(3 * f))
        if f == 0:
            send[2] = pack(0)
            rim2_copies = [
                remote(send.at[2], rim2.at[0, pl.ds(PAD, 96)], rim2_s.at[0], rim2_r.at[0], (ev, after)),
                remote(send.at[2], rim2.at[1, pl.ds(PAD, 96)], rim2_s.at[1], rim2_r.at[1], (ev, before)),
            ]

    st_a = strain(3)
    energy = K[...]
    for c in range(3):
        energy = energy + F[c, PAD : PAD + ROWS, :] * st_a[c]
    elements = fwd_in.shape[-1]
    width = smooth_in.shape[1]
    scale = math.sqrt(width / elements) / STEPS
    twin = jnp.concatenate([proj_in[...], proj_in[...]], axis=0)
    K[...] = energy
    t_hi, t_lo = split(twin)
    k_hi, k_lo = split(K[0:NODES, :])
    blocks = (mm(t_hi, k_hi) + (mm(t_hi, k_lo) + mm(t_lo, k_hi))) * scale
    b_hi, b_lo = split(blocks)
    rows = total * width
    row = lax.broadcasted_iota(jnp.int32, (rows, 128), 0)
    owner = lax.div(row, width)
    tile = width * (lax.rem(owner, e_size) * m_size + lax.div(owner, e_size)) + lax.rem(row, width)
    dest = dest_in[...]
    nt = ((1,), (1,))

    def spread(offset):
        hot = jnp.where(tile + offset == dest, 1.0, 0.0).astype(f32).astype(bf16)
        return mm(hot, b_hi, nt) + mm(hot, b_lo, nt)

    packed = jnp.where(lane < 64, spread(-2), spread(2))
    msg[...] = packed.reshape(m_size, e_size, width, 128)
    a_copies = [
        remote(msg.at[lax.rem(me + o, m_size)], got.at[o - 1], a_s.at[o - 1], a_r.at[o - 1],
               (ev, lax.rem(me + o, m_size)))
        for o in range(1, m_size)
    ]

    st_f = strain(0)
    for c in range(3):
        N[c] = N[c] - time_square * material * st_f[c]
    own_pass(0)

    for copy in a_copies:
        copy.wait_recv()
    mine_sum = msg[me]
    for o in range(m_size - 1):
        mine_sum = mine_sum + got[o]
    part[...] = mine_sum
    b_copies = [
        remote(part.at[lax.rem(ev + o, e_size)], got2.at[o - 1], b_s.at[o - 1], b_r.at[o - 1],
               (lax.rem(ev + o, e_size), me))
        for o in range(1, e_size)
    ]

    for side in range(2):
        rim2_copies[side].wait_recv()
        unpack(rim2.at[side])

    def final(c, t, value):
        N[c, 8 * t : 8 * t + 8, :] = value

    rim_pass(0, rim2, final)
    stores = []
    for c in range(3):
        store = pltpu.make_async_copy(
            N.at[c, pl.ds(0, NODES)], fwd_out.at[pl.ds(NODES * c, NODES), 0], out_s.at[c]
        )
        store.start()
        stores.append(store)

    for copy in coef_copies:
        copy.wait_recv()
    own_coef = pltpu.roll(coef[...], 2, 1)
    left = jnp.where(lin > 0, coef_in[0], 0.0)
    right = jnp.where(lin < total - 1, coef_in[1], 0.0)
    left = jnp.where(lane < 2, pltpu.roll(left, 126, 1), 0.0)
    right = pltpu.roll(right, 6, 1)
    mine[...] = jnp.zeros((128, 128), f32)
    mine[0:8, :] = own_coef + left + right
    coefs = mine[...].T[0:8]

    def smooth(x):
        chain = pltpu.roll(x, 1, 0) + pltpu.roll(x, 7, 0) - 2.0 * x
        new = x + coefs[:, 0:1] * chain
        for d, shift in ((1, 4), (2, 2), (3, 0)):
            digit = lax.shift_right_logical(lane, shift) & 3
            up = jnp.where(digit == 0, 0.0, pltpu.roll(x, 1 << shift, 1))
            down = jnp.where(digit == 3, 0.0, pltpu.roll(x, 128 - (1 << shift), 1))
            new = new + coefs[:, d : d + 1] * (up + down - 2.0 * x)
        return jnp.where(lane < 64, new, 0.0)

    for copy in b_copies:
        copy.wait_recv()
    summed = part[ev]
    for o in range(e_size - 1):
        summed = summed + got2[o]
    x = jnp.concatenate([summed, pltpu.roll(summed, 64, 1)], axis=0)
    x = smooth(smooth(jnp.where(lane < 64, x, 0.0)))
    tiles_out[...] = x[2 : 2 + width, 0:64]

    for store in stores:
        store.wait()
    for copy in rim_copies[0] + rim_copies[1] + rim2_copies + coef_copies + a_copies + b_copies:
        copy.wait_send()


def solution(mesh):
    m_size, e_size = mesh.shape["mesh"], mesh.shape["event"]
    in_specs = (
        P("event", None, None, "mesh"),
        P("event", None, None, "mesh"),
        P(),
        P(),
        P("event", "mesh"),
        P("event", None, "mesh"),
        P("event", "mesh"),
        P("event", "mesh"),
        P(None, ("event", "mesh")),
    )
    out_specs = (P("event", None, None, "mesh"), P(None, ("event", "mesh")))

    def per_device(*args):
        fwd, smoothing = args[0], args[-1]
        width = smoothing.shape[1]
        dma = pltpu.SemaphoreType.DMA
        vmem = pl.BlockSpec(memory_space=pltpu.VMEM)
        hbm = pl.BlockSpec(memory_space=pl.ANY)
        line = (3 * NODES, 1, fwd.shape[-1])
        args = (args[0].reshape(line), args[1].reshape(line), args[2], args[3].T, args[4],
                args[5].reshape(6, 1, fwd.shape[-1]), *args[6:])
        final, tiles = pl.pallas_call(
            functools.partial(kernel, m_size, e_size),
            out_shape=(
                jax.ShapeDtypeStruct(line, f32),
                jax.ShapeDtypeStruct((width, 64), f32),
            ),
            in_specs=[hbm] * 2 + [vmem] * (len(args) - 2),
            out_specs=(hbm, vmem),
            scratch_shapes=[
                pltpu.VMEM((6, 144, 128), f32),
                pltpu.VMEM((6, ROWS, 128), f32),
                pltpu.VMEM((ROWS, 128), f32),
                pltpu.VMEM((ROWS, ROWS), f32),
                pltpu.VMEM((7, ROWS, 128), f32),
                pltpu.VMEM((12, 8, 128), jnp.int32),
                pltpu.VMEM((8, 128), f32),
                pltpu.VMEM((3, 96, 128), f32),
                pltpu.VMEM((2, 2, 144, 128), f32),
                pltpu.VMEM((2, 144, 128), f32),
                pltpu.VMEM((8, 128), f32),
                pltpu.VMEM((2, 8, 128), f32),
                pltpu.VMEM((m_size, e_size, width, 128), f32),
                pltpu.VMEM((e_size, width, 128), f32),
                pltpu.VMEM((m_size - 1, e_size, width, 128), f32),
                pltpu.VMEM((128, 128), f32),
                pltpu.VMEM((e_size - 1, width, 128), f32),
                dma((6,)), dma((3,)), dma((2, 2)), dma((2, 2)), dma((2,)), dma((2,)), dma((2,)), dma((2,)),
                dma((m_size - 1,)), dma((m_size - 1,)), dma((e_size - 1,)), dma((e_size - 1,)),
            ],
            compiler_params=pltpu.CompilerParams(collective_id=0, has_side_effects=True),
        )(*args)
        return final.reshape(fwd.shape), tiles.T

    return jax.shard_map(
        per_device, mesh=mesh, in_specs=in_specs, out_specs=out_specs, check_vma=False
    )
```

```python
import functools
import math

import jax
import jax.numpy as jnp
from jax import lax
from jax.experimental import pallas as pl
from jax.experimental.pallas import tpu as pltpu
from jax.sharding import PartitionSpec as P

STEPS = 2
time_square = 0.4
penalty = 0.5

PAD = 8
ROWS = 128
NODES = 125
SHIFT = (100, -100, 20, -20, 4, -4)
MESH = pl.DeviceIdType.MESH
f32 = jnp.float32
bf16 = jnp.bfloat16


def on_face(face, node):
    i, j, k = node // 25, (node // 5) % 5, node % 5
    return (i == 0, i == 4, j == 0, j == 4, k == 0, k == 4)[face]


TILE_FACES = [
    [f for f in range(6) if any(on_face(f, n) for n in range(8 * t, min(8 * t + 8, NODES)))]
    for t in range(ROWS // 8)
]


def split(x):
    high = x.astype(bf16)
    return high, (x - high.astype(f32)).astype(bf16)


def mm(a, b, dims=((1,), (0,))):
    return lax.dot_general(a, b, (dims, ((), ())), preferred_element_type=f32)


def pick(x, index):
    return jnp.take_along_axis(x, index, axis=1, mode="promise_in_bounds")


def kernel(
    m_size, e_size,
    fwd_in, adj_in, stiff_hbm, proj_hbm, mat_hbm, nb_hbm, dest_hbm, count_hbm, smooth_hbm,
    fwd_out, tiles_out,
    stiff_in, proj_in, mat_in, nb_in, dest_in, count_in, smooth_in,
    F, N, K, S, W, IDX, LIVE, send, rim, rim2, coef, coef_in, msg, part, got, mine, got2,
    in_s, small_s, out_s, rim_s, rim_r, rim2_s, rim2_r, coef_s, coef_r, a_s, a_r, b_s, b_r, rounds,
):
    me = lax.axis_index("mesh")
    ev = lax.axis_index("event")
    total = m_size * e_size
    lin = ev * m_size + me
    after = lax.rem(me + 1, m_size)
    before = lax.rem(me + m_size - 1, m_size)

    barrier = pltpu.get_barrier_semaphore()
    core = lax.rem(ev, 2)
    chip = lax.div(ev, 2)
    chips = e_size // 2
    near = [((2 * chip + 1 - core, me), None)]
    for step in (1, -1):
        inside = (chip + step >= 0) & (chip + step < chips)
        near += [((2 * (chip + step) + c, me), inside) for c in range(2)]
    near_count = 1 + 2 * ((chip > 0).astype(jnp.int32) + (chip < chips - 1).astype(jnp.int32))

    def greet(sem):
        for device, inside in near:
            if inside is None:
                pl.semaphore_signal(sem, inc=1, device_id=device, device_id_type=MESH)
            else:

                @pl.when(inside)
                def _():
                    pl.semaphore_signal(sem, inc=1, device_id=device, device_id_type=MESH)

    for o in range(1, m_size):
        pl.semaphore_signal(
            barrier, inc=1, device_id=(ev, lax.rem(me + o, m_size)), device_id_type=MESH
        )
    greet(barrier)

    loads = []
    for fc in range(6):
        source = fwd_in if fc < 3 else adj_in
        load = pltpu.make_async_copy(
            source.at[pl.ds(NODES * (fc % 3), NODES), 0], F.at[fc, pl.ds(PAD, NODES)], in_s.at[fc]
        )
        load.start()
        loads.append(load)

    small = []
    for n, (src, dst) in enumerate((
        (smooth_hbm, smooth_in), (stiff_hbm, stiff_in), (nb_hbm, nb_in), (count_hbm, count_in),
        (mat_hbm, mat_in), (proj_hbm, proj_in), (dest_hbm, dest_in),
    )):
        load = pltpu.make_async_copy(src, dst, small_s.at[n])
        load.start()
        small.append(load)

    lane = lax.broadcasted_iota(jnp.int32, (1, 128), 1)
    zero8 = jnp.zeros((PAD, 128), f32)
    for fc in range(6):
        F[fc, 0:PAD, :] = zero8
        F[fc, PAD + NODES : 144, :] = jnp.zeros((144 - PAD - NODES, 128), f32)

    def pack(base):
        wide = [F[base + c, PAD : PAD + ROWS, :] for c in range(3)]
        head = jnp.where(
            lane < 32,
            wide[0][:96],
            jnp.where(lane < 64, pltpu.roll(wide[1][:96], 32, 1), pltpu.roll(wide[2][:96], 64, 1)),
        )
        tail = pltpu.roll(jnp.concatenate([w[96:] for w in wide], axis=0), 96, 1)
        return jnp.where(lane < 96, head, tail)

    for f in range(2):
        for load in loads[3 * f : 3 * f + 3]:
            load.wait()
        send[f] = pack(3 * f)
    coef[...] = jnp.zeros((8, 128), f32)
    small[0].wait()
    coef[0:4, 0:4] = smooth_in[...]

    pl.semaphore_wait(barrier, near_count + (m_size - 1))

    def remote(src, dst, s, r, device):
        copy = pltpu.make_async_remote_copy(
            src_ref=src, dst_ref=dst, send_sem=s, recv_sem=r, device_id=device, device_id_type=MESH
        )
        copy.start()
        return copy

    rim_copies = [
        [
            remote(send.at[f], rim.at[f, 0, pl.ds(PAD, 96)], rim_s.at[f, 0], rim_r.at[f, 0], (ev, after)),
            remote(send.at[f], rim.at[f, 1, pl.ds(PAD, 96)], rim_s.at[f, 1], rim_r.at[f, 1], (ev, before)),
        ]
        for f in range(2)
    ]
    coef_copies = [
        remote(coef, coef_in.at[0], coef_s.at[0], coef_r.at[0], (ev, after)),
        remote(coef, coef_in.at[1], coef_s.at[1], coef_r.at[1], (ev, before)),
    ]
    if chips > 2:
        greet(rounds.at[0])

    for load in small[1:]:
        load.wait()
    live = jnp.where(lane < count_in[0:1, 0:1], 1.0, 0.0).astype(f32)
    LIVE[...] = jnp.broadcast_to(live, (8, 128))
    for fc in range(6):
        F[fc, PAD : PAD + NODES, :] = F[fc, PAD : PAD + NODES, :] * live

    node = lax.broadcasted_iota(jnp.int32, (ROWS, 128), 0).astype(f32)
    i = jnp.floor((node + 0.5) / 25.0)
    rest = node - 25.0 * i
    j = jnp.floor((rest + 0.5) / 5.0)
    k = rest - 5.0 * j
    count = jnp.zeros((ROWS, 128), f32)
    for f, test in enumerate((i == 0.0, i == 4.0, j == 0.0, j == 4.0, k == 0.0, k == 4.0)):
        mask = jnp.where(test & (node < NODES - 0.5), 1.0, 0.0).astype(f32)
        W[f] = mask
        count = count + mask
    W[6] = count
    nb = nb_in[:, 0, :]
    target = lax.shift_right_logical(nb, 7)
    slot = nb & 127
    relative = lax.rem(target - me + m_size, m_size)
    for f in range(6):
        IDX[f] = jnp.broadcast_to(slot[f : f + 1], (8, 128))
        IDX[6 + f] = jnp.broadcast_to(relative[f : f + 1], (8, 128))
    S[...] = jnp.zeros((ROWS, ROWS), f32)
    S[0:NODES, 0:NODES] = stiff_in[...]
    s_hi, s_lo = split(S[...])
    material = mat_in[...]

    def strain(base):
        wide = jnp.concatenate([F[base + c, PAD : PAD + ROWS, :] for c in range(3)], axis=1)
        hi, lo = split(wide)
        both = mm(s_hi, hi) + (mm(s_hi, lo) + mm(s_lo, hi))
        return [both[:, 128 * c : 128 * (c + 1)] for c in range(3)]

    def own_pass(base):
        def body(c, carry):
            for t in range(ROWS // 8):
                acc = jnp.zeros((8, 128), f32)
                for f in TILE_FACES[t]:
                    x = F[base + c, 8 * t + PAD + SHIFT[f] : 8 * t + 2 * PAD + SHIFT[f], :]
                    g = pick(x, IDX[f])
                    acc = acc + jnp.where(IDX[6 + f] == 0, g, 0.0) * W[f, 8 * t : 8 * t + 8, :]
                v = F[base + c, 8 * t + PAD : 8 * t + 2 * PAD, :]
                acc = acc - W[6, 8 * t : 8 * t + 8, :] * v
                N[base + c, 8 * t : 8 * t + 8, :] = (
                    N[base + c, 8 * t : 8 * t + 8, :] + (time_square * penalty) * acc
                )
            return carry

        lax.fori_loop(0, 3, body, 0)

    def unpack(ref):
        pieces = [
            pltpu.roll(ref[PAD + 32 * c : PAD + 32 * c + 32, :], 32 * (c + 1), 1) for c in range(3)
        ]
        ref[PAD + 96 : PAD + 128, :] = jnp.where(
            lane < 32, pieces[0], jnp.where(lane < 64, pieces[1], pieces[2])
        )
        ref[0:PAD, :] = zero8
        ref[PAD + 128 : PAD + 136, :] = zero8

    def rim_pass(base, ref, store):
        def body(c, carry):
            live8 = LIVE[...]
            for t in range(ROWS // 8):
                acc = jnp.zeros((8, 128), f32)
                for f in TILE_FACES[t]:
                    low = 8 * t + PAD + SHIFT[f]
                    at = (IDX[f] & 31) + 32 * c
                    r = IDX[6 + f]
                    g = jnp.where(
                        r == 1, pick(ref[1, low : low + 8, :], at), pick(ref[0, low : low + 8, :], at)
                    )
                    acc = acc + jnp.where(r == 0, 0.0, g) * W[f, 8 * t : 8 * t + 8, :]
                old = N[base + c, 8 * t : 8 * t + 8, :]
                store(c, t, live8 * (old + (time_square * penalty) * acc))
            return carry

        lax.fori_loop(0, 3, body, 0)

    st_f = strain(0)
    st_a = strain(3)
    energy = jnp.zeros((ROWS, 128), f32)
    for c in range(3):
        vf = F[c, PAD : PAD + ROWS, :]
        energy = energy + vf * st_a[c]
        N[c] = vf - time_square * material * st_f[c]
        N[3 + c] = F[3 + c, PAD : PAD + ROWS, :] - time_square * material * st_a[c]
    K[...] = energy
    own_pass(0)
    for n in range(chips - 2):
        pl.semaphore_wait(rounds.at[n], near_count)
        if n + 1 < chips - 2:
            greet(rounds.at[n + 1])
        if n == 0:
            own_pass(3)
    if chips <= 2:
        own_pass(3)

    def keep(base):
        def store(c, t, value):
            at = pl.ds(8 * t + PAD, 8)
            if base == 0:
                N[c, 8 * t : 8 * t + 8, :] = 2.0 * value - F[c, at, :]
            F[base + c, at, :] = value

        return store

    for f in range(2):
        for side in range(2):
            rim_copies[f][side].wait_recv()
            unpack(rim.at[f, side])
        rim_pass(3 * f, rim.at[f], keep(3 * f))
        if f == 0:
            send[2] = pack(0)

    st_a = strain(3)
    energy = K[...]
    for c in range(3):
        energy = energy + F[c, PAD : PAD + ROWS, :] * st_a[c]
    elements = F.shape[-1]
    width = smooth_in.shape[1]
    scale = math.sqrt(width / elements) / STEPS
    twin = jnp.concatenate([proj_in[...], proj_in[...]], axis=0)
    K[...] = energy
    t_hi, t_lo = split(twin)
    k_hi, k_lo = split(K[0:NODES, :])
    blocks = (mm(t_hi, k_hi) + (mm(t_hi, k_lo) + mm(t_lo, k_hi))) * scale
    b_hi, b_lo = split(blocks)
    rows = total * width
    row = lax.broadcasted_iota(jnp.int32, (rows, 128), 0)
    owner = lax.div(row, width)
    tile = width * (lax.rem(owner, e_size) * m_size + lax.div(owner, e_size)) + lax.rem(row, width)
    dest = dest_in[...]
    nt = ((1,), (1,))

    def spread(offset):
        hot = jnp.where(tile + offset == dest, 1.0, 0.0).astype(f32).astype(bf16)
        return mm(hot, b_hi, nt) + mm(hot, b_lo, nt)

    packed = jnp.where(lane < 64, spread(-2), spread(2))
    msg[...] = packed.reshape(m_size, e_size, width, 128)
    a_copies = [
        remote(msg.at[lax.rem(me + o, m_size)], got.at[o - 1], a_s.at[o - 1], a_r.at[o - 1],
               (ev, lax.rem(me + o, m_size)))
        for o in range(1, m_size)
    ]

    rim2_copies = [
        remote(send.at[2], rim2.at[0, pl.ds(PAD, 96)], rim2_s.at[0], rim2_r.at[0], (ev, after)),
        remote(send.at[2], rim2.at[1, pl.ds(PAD, 96)], rim2_s.at[1], rim2_r.at[1], (ev, before)),
    ]

    st_f = strain(0)
    for c in range(3):
        N[c] = N[c] - time_square * material * st_f[c]
    own_pass(0)

    for copy in coef_copies:
        copy.wait_recv()
    coef_copies += [
        remote(coef_in.at[0], coef_in.at[2], coef_s.at[2], coef_r.at[2],
               (lax.rem(ev + 1, e_size), me)),
        remote(coef_in.at[1], coef_in.at[3], coef_s.at[3], coef_r.at[3],
               (lax.rem(ev + e_size - 1, e_size), me)),
    ]
    for copy in a_copies:
        copy.wait_recv()
    mine_sum = msg[me]
    for o in range(m_size - 1):
        mine_sum = mine_sum + got[o]
    part[...] = mine_sum
    b_copies = [
        remote(part.at[lax.rem(ev + o, e_size)], got2.at[o - 1], b_s.at[o - 1], b_r.at[o - 1],
               (lax.rem(ev + o, e_size), me))
        for o in range(1, e_size)
    ]

    for side in range(2):
        rim2_copies[side].wait_recv()
        unpack(rim2.at[side])

    def final(c, t, value):
        N[c, 8 * t : 8 * t + 8, :] = value

    rim_pass(0, rim2, final)
    stores = []
    for c in range(3):
        store = pltpu.make_async_copy(
            N.at[c, pl.ds(0, NODES)], fwd_out.at[pl.ds(NODES * c, NODES), 0], out_s.at[c]
        )
        store.start()
        stores.append(store)

    for copy in coef_copies[2:]:
        copy.wait_recv()
    own_coef = pltpu.roll(coef[...], 2, 1)
    left = jnp.where(lin > 0, jnp.where(me > 0, coef_in[0], coef_in[2]), 0.0)
    right = jnp.where(
        lin < total - 1, jnp.where(me < m_size - 1, coef_in[1], coef_in[3]), 0.0
    )
    left = jnp.where(lane < 2, pltpu.roll(left, 126, 1), 0.0)
    right = pltpu.roll(right, 6, 1)
    mine[...] = jnp.zeros((128, 128), f32)
    mine[0:8, :] = own_coef + left + right
    coefs = mine[...].T[0:8]

    def smooth(x):
        chain = pltpu.roll(x, 1, 0) + pltpu.roll(x, 7, 0) - 2.0 * x
        new = x + coefs[:, 0:1] * chain
        for d, shift in ((1, 4), (2, 2), (3, 0)):
            digit = lax.shift_right_logical(lane, shift) & 3
            up = jnp.where(digit == 0, 0.0, pltpu.roll(x, 1 << shift, 1))
            down = jnp.where(digit == 3, 0.0, pltpu.roll(x, 128 - (1 << shift), 1))
            new = new + coefs[:, d : d + 1] * (up + down - 2.0 * x)
        return jnp.where(lane < 64, new, 0.0)

    for copy in b_copies:
        copy.wait_recv()
    summed = part[ev]
    for o in range(e_size - 1):
        summed = summed + got2[o]
    x = jnp.concatenate([summed, pltpu.roll(summed, 64, 1)], axis=0)
    x = smooth(smooth(jnp.where(lane < 64, x, 0.0)))
    tiles_out[...] = x[2 : 2 + width, 0:64]

    for store in stores:
        store.wait()
    for copy in rim_copies[0] + rim_copies[1] + rim2_copies + coef_copies + a_copies + b_copies:
        copy.wait_send()


def solution(mesh):
    m_size, e_size = mesh.shape["mesh"], mesh.shape["event"]
    in_specs = (
        P("event", None, None, "mesh"),
        P("event", None, None, "mesh"),
        P(),
        P(),
        P("event", "mesh"),
        P("event", None, "mesh"),
        P("event", "mesh"),
        P("event", "mesh"),
        P(None, ("event", "mesh")),
    )
    out_specs = (P("event", None, None, "mesh"), P(None, ("event", "mesh")))

    def per_device(*args):
        fwd, smoothing = args[0], args[-1]
        width = smoothing.shape[1]
        dma = pltpu.SemaphoreType.DMA
        vmem = pl.BlockSpec(memory_space=pltpu.VMEM)
        hbm = pl.BlockSpec(memory_space=pltpu.HBM)
        line = (3 * NODES, 1, fwd.shape[-1])
        args = (args[0].reshape(line), args[1].reshape(line), args[2], args[3].T, args[4],
                args[5].reshape(6, 1, fwd.shape[-1]), *args[6:])
        final, tiles = pl.pallas_call(
            functools.partial(kernel, m_size, e_size),
            out_shape=(
                pltpu.VMEM(line, f32),
                pltpu.VMEM((width, 64), f32),
            ),
            in_specs=[hbm] * len(args),
            out_specs=(vmem, vmem),
            scratch_shapes=[pltpu.VMEM(x.shape, x.dtype) for x in args[2:]]
            + [
                pltpu.VMEM((6, 144, 128), f32),
                pltpu.VMEM((6, ROWS, 128), f32),
                pltpu.VMEM((ROWS, 128), f32),
                pltpu.VMEM((ROWS, ROWS), f32),
                pltpu.VMEM((7, ROWS, 128), f32),
                pltpu.VMEM((12, 8, 128), jnp.int32),
                pltpu.VMEM((8, 128), f32),
                pltpu.VMEM((3, 96, 128), f32),
                pltpu.VMEM((2, 2, 144, 128), f32),
                pltpu.VMEM((2, 144, 128), f32),
                pltpu.VMEM((8, 128), f32),
                pltpu.VMEM((4, 8, 128), f32),
                pltpu.VMEM((m_size, e_size, width, 128), f32),
                pltpu.VMEM((e_size, width, 128), f32),
                pltpu.VMEM((m_size - 1, e_size, width, 128), f32),
                pltpu.VMEM((128, 128), f32),
                pltpu.VMEM((e_size - 1, width, 128), f32),
                dma((6,)), dma((7,)), dma((3,)), dma((2, 2)), dma((2, 2)), dma((2,)), dma((2,)), dma((4,)), dma((4,)),
                dma((m_size - 1,)), dma((m_size - 1,)), dma((e_size - 1,)), dma((e_size - 1,)),
                pltpu.SemaphoreType.REGULAR((max(e_size // 2 - 2, 1),)),
            ],
            compiler_params=pltpu.CompilerParams(collective_id=0, has_side_effects=True),
        )(*args)
        return final.reshape(fwd.shape), tiles.T

    return jax.shard_map(
        per_device, mesh=mesh, in_specs=in_specs, out_specs=out_specs, check_vma=False
    )
```

```python
import functools
import math

import jax
import jax.numpy as jnp
from jax import lax
from jax.experimental import pallas as pl
from jax.experimental.pallas import tpu as pltpu
from jax.sharding import PartitionSpec as P

STEPS = 2
time_square = 0.4
penalty = 0.5

PAD = 8
ROWS = 128
NODES = 125
SHIFT = (100, -100, 20, -20, 4, -4)
MESH = pl.DeviceIdType.MESH
f32 = jnp.float32
bf16 = jnp.bfloat16


def on_face(face, node):
    i, j, k = node // 25, (node // 5) % 5, node % 5
    return (i == 0, i == 4, j == 0, j == 4, k == 0, k == 4)[face]


TILE_FACES = [
    [f for f in range(6) if any(on_face(f, n) for n in range(8 * t, min(8 * t + 8, NODES)))]
    for t in range(ROWS // 8)
]


def split(x):
    high = x.astype(bf16)
    return high, (x - high.astype(f32)).astype(bf16)


def mm(a, b, dims=((1,), (0,))):
    return lax.dot_general(a, b, (dims, ((), ())), preferred_element_type=f32)


def pick(x, index):
    return jnp.take_along_axis(x, index, axis=1, mode="promise_in_bounds")


def kernel(
    m_size, e_size,
    fwd_in, adj_in, stiff_hbm, proj_hbm, mat_hbm, nb_hbm, dest_hbm, count_hbm, smooth_hbm,
    fwd_out, tiles_out,
    stiff_in, proj_in, mat_in, nb_in, dest_in, count_in, smooth_in,
    F, N, K, S, W, IDX, LIVE, send, rim, rim2, coef, coef_in, msg, part, got, mine, got2,
    in_s, small_s, out_s, rim_s, rim_r, rim2_s, rim2_r, coef_s, coef_r, a_s, a_r, b_s, b_r, rounds,
):
    me = lax.axis_index("mesh")
    ev = lax.axis_index("event")
    total = m_size * e_size
    lin = ev * m_size + me
    after = lax.rem(me + 1, m_size)
    before = lax.rem(me + m_size - 1, m_size)

    barrier = pltpu.get_barrier_semaphore()
    core = lax.rem(ev, 2)
    chip = lax.div(ev, 2)
    chips = e_size // 2
    near = [((2 * chip + 1 - core, me), None)]
    for step in (1, -1):
        inside = (chip + step >= 0) & (chip + step < chips)
        near += [((2 * (chip + step) + c, me), inside) for c in range(2)]
    near_count = 1 + 2 * ((chip > 0).astype(jnp.int32) + (chip < chips - 1).astype(jnp.int32))

    def greet(sem):
        for device, inside in near:
            if inside is None:
                pl.semaphore_signal(sem, inc=1, device_id=device, device_id_type=MESH)
            else:

                @pl.when(inside)
                def _():
                    pl.semaphore_signal(sem, inc=1, device_id=device, device_id_type=MESH)

    for o in range(1, m_size):
        pl.semaphore_signal(
            barrier, inc=1, device_id=(ev, lax.rem(me + o, m_size)), device_id_type=MESH
        )
    greet(barrier)

    loads = []
    for fc in range(6):
        source = fwd_in if fc < 3 else adj_in
        load = pltpu.make_async_copy(
            source.at[pl.ds(NODES * (fc % 3), NODES), 0], F.at[fc, pl.ds(PAD, NODES)], in_s.at[fc]
        )
        load.start()
        loads.append(load)

    small = []
    for n, (src, dst) in enumerate((
        (smooth_hbm, smooth_in), (stiff_hbm, stiff_in), (nb_hbm, nb_in), (count_hbm, count_in),
        (mat_hbm, mat_in), (proj_hbm, proj_in), (dest_hbm, dest_in),
    )):
        load = pltpu.make_async_copy(src, dst, small_s.at[n])
        load.start()
        small.append(load)

    lane = lax.broadcasted_iota(jnp.int32, (1, 128), 1)
    zero8 = jnp.zeros((PAD, 128), f32)
    for fc in range(6):
        F[fc, 0:PAD, :] = zero8
        F[fc, PAD + NODES : 144, :] = jnp.zeros((144 - PAD - NODES, 128), f32)

    def pack(base):
        wide = [F[base + c, PAD : PAD + ROWS, :] for c in range(3)]
        head = jnp.where(
            lane < 32,
            wide[0][:96],
            jnp.where(lane < 64, pltpu.roll(wide[1][:96], 32, 1), pltpu.roll(wide[2][:96], 64, 1)),
        )
        tail = pltpu.roll(jnp.concatenate([w[96:] for w in wide], axis=0), 96, 1)
        return jnp.where(lane < 96, head, tail)

    for f in range(2):
        for load in loads[3 * f : 3 * f + 3]:
            load.wait()
        send[f] = pack(3 * f)
    coef[...] = jnp.zeros((8, 128), f32)
    small[0].wait()
    coef[0:4, 0:4] = smooth_in[...]

    pl.semaphore_wait(barrier, near_count + (m_size - 1))

    def remote(src, dst, s, r, device):
        copy = pltpu.make_async_remote_copy(
            src_ref=src, dst_ref=dst, send_sem=s, recv_sem=r, device_id=device, device_id_type=MESH
        )
        copy.start()
        return copy

    paired = m_size == 4
    first = 1 - lax.rem(me, 2) if paired else 0
    second = 1 - first
    rows = pl.ds(PAD, 96)

    def to_sides(src, land, sends, recvs):
        slots = (second, first) if paired else (first, second)
        return [
            remote(src, land.at[slot, rows], sends.at[n], recvs.at[n],
                   (ev, jnp.where(slot == 0, after, before)))
            for n, slot in enumerate(slots)
        ]

    rim_copies = [
        to_sides(send.at[0], rim.at[0], rim_s.at[0], rim_r.at[0]),
        to_sides(send.at[1], rim.at[1], rim_s.at[1], rim_r.at[1]),
    ]
    coef_copies = [
        remote(coef, coef_in.at[0], coef_s.at[0], coef_r.at[0], (ev, after)),
        remote(coef, coef_in.at[1], coef_s.at[1], coef_r.at[1], (ev, before)),
    ]
    if chips > 2:
        greet(rounds.at[0])

    for load in small[1:]:
        load.wait()
    live = jnp.where(lane < count_in[0:1, 0:1], 1.0, 0.0).astype(f32)
    LIVE[...] = jnp.broadcast_to(live, (8, 128))
    for fc in range(6):
        F[fc, PAD : PAD + NODES, :] = F[fc, PAD : PAD + NODES, :] * live

    node = lax.broadcasted_iota(jnp.int32, (ROWS, 128), 0).astype(f32)
    i = jnp.floor((node + 0.5) / 25.0)
    rest = node - 25.0 * i
    j = jnp.floor((rest + 0.5) / 5.0)
    k = rest - 5.0 * j
    count = jnp.zeros((ROWS, 128), f32)
    for f, test in enumerate((i == 0.0, i == 4.0, j == 0.0, j == 4.0, k == 0.0, k == 4.0)):
        mask = jnp.where(test & (node < NODES - 0.5), 1.0, 0.0).astype(f32)
        W[f] = mask
        count = count + mask
    W[6] = count
    nb = nb_in[:, 0, :]
    target = lax.shift_right_logical(nb, 7)
    slot = nb & 127
    relative = lax.rem(target - me + m_size, m_size)
    for f in range(6):
        IDX[f] = jnp.broadcast_to(slot[f : f + 1], (8, 128))
        IDX[6 + f] = jnp.broadcast_to(relative[f : f + 1], (8, 128))
    S[...] = jnp.zeros((ROWS, ROWS), f32)
    S[0:NODES, 0:NODES] = stiff_in[...]
    s_hi, s_lo = split(S[...])
    material = mat_in[...]

    def strain(base):
        wide = jnp.concatenate([F[base + c, PAD : PAD + ROWS, :] for c in range(3)], axis=1)
        hi, lo = split(wide)
        both = mm(s_hi, hi) + (mm(s_hi, lo) + mm(s_lo, hi))
        return [both[:, 128 * c : 128 * (c + 1)] for c in range(3)]

    def face_sums(read, offset, relative_to):
        sums = [None] * (ROWS // 8)
        for f in range(6):
            at = IDX[f] if offset is None else (IDX[f] & 31) + offset
            here = IDX[6 + f] == relative_to
            for t in range(ROWS // 8):
                if f in TILE_FACES[t]:
                    g = jnp.where(here, pick(read(8 * t + PAD + SHIFT[f]), at), 0.0)
                    g = g * W[f, 8 * t : 8 * t + 8, :]
                    sums[t] = g if sums[t] is None else sums[t] + g
        return sums

    def own_pass(base):
        def body(c, carry):
            sums = face_sums(lambda low: F[base + c, low : low + 8, :], None, 0)
            for t in range(ROWS // 8):
                at = pl.ds(8 * t, 8)
                v = F[base + c, 8 * t + PAD : 8 * t + 2 * PAD, :]
                acc = sums[t] - W[6, at, :] * v
                N[base + c, at, :] = N[base + c, at, :] + (time_square * penalty) * acc
            return carry

        lax.fori_loop(0, 3, body, 0)

    def unpack(ref):
        pieces = [
            pltpu.roll(ref[PAD + 32 * c : PAD + 32 * c + 32, :], 32 * (c + 1), 1) for c in range(3)
        ]
        ref[PAD + 96 : PAD + 128, :] = jnp.where(
            lane < 32, pieces[0], jnp.where(lane < 64, pieces[1], pieces[2])
        )
        ref[0:PAD, :] = zero8
        ref[PAD + 128 : PAD + 136, :] = zero8

    def rim_pass(base, ref, side, store):
        relative_to = jnp.where(side == 1, 1, m_size - 1)

        def body(c, carry):
            sums = face_sums(lambda low: ref[low : low + 8, :], 32 * c, relative_to)
            for t in range(ROWS // 8):
                old = N[base + c, 8 * t : 8 * t + 8, :]
                store(c, t, old + (time_square * penalty) * sums[t])
            return carry

        lax.fori_loop(0, 3, body, 0)

    def add(base):
        def store(c, t, value):
            N[base + c, 8 * t : 8 * t + 8, :] = value

        return store

    st_f = strain(0)
    st_a = strain(3)
    energy = jnp.zeros((ROWS, 128), f32)
    for c in range(3):
        vf = F[c, PAD : PAD + ROWS, :]
        energy = energy + vf * st_a[c]
        N[c] = vf - time_square * material * st_f[c]
        N[3 + c] = F[3 + c, PAD : PAD + ROWS, :] - time_square * material * st_a[c]
    K[...] = energy
    own_pass(0)
    for n in range(chips - 2):
        pl.semaphore_wait(rounds.at[n], near_count)
        if n + 1 < chips - 2:
            greet(rounds.at[n + 1])
        if n == 0:
            own_pass(3)
    if chips <= 2:
        own_pass(3)

    def keep(base):
        def store(c, t, value):
            value = LIVE[...] * value
            at = pl.ds(8 * t + PAD, 8)
            if base == 0:
                N[c, 8 * t : 8 * t + 8, :] = 2.0 * value - F[c, at, :]
            F[base + c, at, :] = value

        return store

    for f in range(2):
        rim_copies[f][0].wait_recv()
        near_ref = rim.at[f, first]
        unpack(near_ref)
        rim_pass(3 * f, near_ref, first, add(3 * f))
    for f in range(2):
        rim_copies[f][1].wait_recv()
        far_ref = rim.at[f, second]
        unpack(far_ref)
        rim_pass(3 * f, far_ref, second, keep(3 * f))
        if f == 0:
            send[2] = pack(0)

    st_a = strain(3)
    energy = K[...]
    for c in range(3):
        energy = energy + F[c, PAD : PAD + ROWS, :] * st_a[c]
    elements = F.shape[-1]
    width = smooth_in.shape[1]
    scale = math.sqrt(width / elements) / STEPS
    twin = jnp.concatenate([proj_in[...], proj_in[...]], axis=0)
    K[...] = energy
    t_hi, t_lo = split(twin)
    k_hi, k_lo = split(K[0:NODES, :])
    blocks = (mm(t_hi, k_hi) + (mm(t_hi, k_lo) + mm(t_lo, k_hi))) * scale
    b_hi, b_lo = split(blocks)
    row = lax.broadcasted_iota(jnp.int32, (total * width, 128), 0)
    owner = lax.div(row, width)
    tile = width * (lax.rem(owner, e_size) * m_size + lax.div(owner, e_size)) + lax.rem(row, width)
    dest = dest_in[...]
    nt = ((1,), (1,))

    def spread(offset):
        hot = jnp.where(tile + offset == dest, 1.0, 0.0).astype(f32).astype(bf16)
        return mm(hot, b_hi, nt) + mm(hot, b_lo, nt)

    packed = jnp.where(lane < 64, spread(-2), spread(2))
    msg[...] = packed.reshape(m_size, e_size, width, 128)
    a_copies = [
        remote(msg.at[lax.rem(me + o, m_size)], got.at[o - 1], a_s.at[o - 1], a_r.at[o - 1],
               (ev, lax.rem(me + o, m_size)))
        for o in range(1, m_size)
    ]

    rim2_copies = to_sides(send.at[2], rim2, rim2_s, rim2_r)

    st_f = strain(0)
    for c in range(3):
        N[c] = N[c] - time_square * material * st_f[c]
    own_pass(0)

    for copy in coef_copies:
        copy.wait_recv()
    coef_copies += [
        remote(coef_in.at[0], coef_in.at[2], coef_s.at[2], coef_r.at[2],
               (lax.rem(ev + 1, e_size), me)),
        remote(coef_in.at[1], coef_in.at[3], coef_s.at[3], coef_r.at[3],
               (lax.rem(ev + e_size - 1, e_size), me)),
    ]
    for copy in a_copies:
        copy.wait_recv()
    mine_sum = msg[me]
    for o in range(m_size - 1):
        mine_sum = mine_sum + got[o]
    part[...] = mine_sum
    b_copies = [
        remote(part.at[lax.rem(ev + o, e_size)], got2.at[o - 1], b_s.at[o - 1], b_r.at[o - 1],
               (lax.rem(ev + o, e_size), me))
        for o in range(1, e_size)
    ]

    def final(c, t, value):
        N[c, 8 * t : 8 * t + 8, :] = LIVE[...] * value

    for n, side in enumerate((first, second)):
        rim2_copies[n].wait_recv()
        ref = rim2.at[side]
        unpack(ref)
        rim_pass(0, ref, side, add(0) if n == 0 else final)
    stores = []
    for c in range(3):
        store = pltpu.make_async_copy(
            N.at[c, pl.ds(0, NODES)], fwd_out.at[pl.ds(NODES * c, NODES), 0], out_s.at[c]
        )
        store.start()
        stores.append(store)

    for copy in coef_copies[2:]:
        copy.wait_recv()
    own_coef = pltpu.roll(coef[...], 2, 1)
    left = jnp.where(lin > 0, jnp.where(me > 0, coef_in[0], coef_in[2]), 0.0)
    right = jnp.where(
        lin < total - 1, jnp.where(me < m_size - 1, coef_in[1], coef_in[3]), 0.0
    )
    left = jnp.where(lane < 2, pltpu.roll(left, 126, 1), 0.0)
    right = pltpu.roll(right, 6, 1)
    mine[...] = jnp.zeros((128, 128), f32)
    mine[0:8, :] = own_coef + left + right
    coefs = mine[...].T[0:8]

    def smooth(x):
        chain = pltpu.roll(x, 1, 0) + pltpu.roll(x, 7, 0) - 2.0 * x
        new = x + coefs[:, 0:1] * chain
        for d, shift in ((1, 4), (2, 2), (3, 0)):
            digit = lax.shift_right_logical(lane, shift) & 3
            up = jnp.where(digit == 0, 0.0, pltpu.roll(x, 1 << shift, 1))
            down = jnp.where(digit == 3, 0.0, pltpu.roll(x, 128 - (1 << shift), 1))
            new = new + coefs[:, d : d + 1] * (up + down - 2.0 * x)
        return jnp.where(lane < 64, new, 0.0)

    for copy in b_copies:
        copy.wait_recv()
    summed = part[ev]
    for o in range(e_size - 1):
        summed = summed + got2[o]
    x = jnp.concatenate([summed, pltpu.roll(summed, 64, 1)], axis=0)
    x = smooth(smooth(jnp.where(lane < 64, x, 0.0)))
    tiles_out[...] = x[2 : 2 + width, 0:64]

    for store in stores:
        store.wait()
    for copy in rim_copies[0] + rim_copies[1] + rim2_copies + coef_copies + a_copies + b_copies:
        copy.wait_send()


def solution(mesh):
    m_size, e_size = mesh.shape["mesh"], mesh.shape["event"]
    in_specs = (
        P("event", None, None, "mesh"),
        P("event", None, None, "mesh"),
        P(),
        P(),
        P("event", "mesh"),
        P("event", None, "mesh"),
        P("event", "mesh"),
        P("event", "mesh"),
        P(None, ("event", "mesh")),
    )
    out_specs = (P("event", None, None, "mesh"), P(None, ("event", "mesh")))

    def per_device(*args):
        fwd, smoothing = args[0], args[-1]
        width = smoothing.shape[1]
        dma = pltpu.SemaphoreType.DMA
        vmem = pl.BlockSpec(memory_space=pltpu.VMEM)
        hbm = pl.BlockSpec(memory_space=pltpu.HBM)
        line = (3 * NODES, 1, fwd.shape[-1])
        args = (args[0].reshape(line), args[1].reshape(line), args[2], args[3].T, args[4],
                args[5].reshape(6, 1, fwd.shape[-1]), *args[6:])
        final, tiles = pl.pallas_call(
            functools.partial(kernel, m_size, e_size),
            out_shape=(
                pltpu.VMEM(line, f32),
                pltpu.VMEM((width, 64), f32),
            ),
            in_specs=[hbm] * len(args),
            out_specs=(vmem, vmem),
            scratch_shapes=[pltpu.VMEM(x.shape, x.dtype) for x in args[2:]]
            + [
                pltpu.VMEM((6, 144, 128), f32),
                pltpu.VMEM((6, ROWS, 128), f32),
                pltpu.VMEM((ROWS, 128), f32),
                pltpu.VMEM((ROWS, ROWS), f32),
                pltpu.VMEM((7, ROWS, 128), f32),
                pltpu.VMEM((12, 8, 128), jnp.int32),
                pltpu.VMEM((8, 128), f32),
                pltpu.VMEM((3, 96, 128), f32),
                pltpu.VMEM((2, 2, 144, 128), f32),
                pltpu.VMEM((2, 144, 128), f32),
                pltpu.VMEM((8, 128), f32),
                pltpu.VMEM((4, 8, 128), f32),
                pltpu.VMEM((m_size, e_size, width, 128), f32),
                pltpu.VMEM((e_size, width, 128), f32),
                pltpu.VMEM((m_size - 1, e_size, width, 128), f32),
                pltpu.VMEM((128, 128), f32),
                pltpu.VMEM((e_size - 1, width, 128), f32),
                dma((6,)), dma((7,)), dma((3,)), dma((2, 2)), dma((2, 2)), dma((2,)), dma((2,)), dma((4,)), dma((4,)),
                dma((m_size - 1,)), dma((m_size - 1,)), dma((e_size - 1,)), dma((e_size - 1,)),
                pltpu.SemaphoreType.REGULAR((max(e_size // 2 - 2, 1),)),
            ],
            compiler_params=pltpu.CompilerParams(collective_id=0, has_side_effects=True),
        )(*args)
        return final.reshape(fwd.shape), tiles.T

    return jax.shard_map(
        per_device, mesh=mesh, in_specs=in_specs, out_specs=out_specs, check_vma=False
    )
```
